32 devices in a mesh: wide: 4 (over x, core), narrow: 8 (over z, y).
Axes of the slice: x: 2, y: 2, z: 4, core: 2. Of those that a mesh axis runs over, the one named last changes fastest.
Arguments:
- activations: bfloat16 [4, 32, 32, 1920], P(None, 'wide', None, 'narrow'), may hold values from -6 to 6
- covariance: float32 [17280, 17280], P('wide', 'narrow'), may hold values from -0.06 to 3, as said below
Outputs:
- updated: float32 [17280, 17280], P('wide', 'narrow')
The draws below stay inside these ranges and needn't reach their ends.
Inputs may be any that keep to these rules, and one draw needn't show every extreme that they name: `covariance`: symmetric.
All inputs are finite; a program needn't handle non-finite values.
Results may differ from the reference program's by a relative error of at most 0.0003.
Values may be sent and summed in bfloat16 or wider, within the bound.
A program may use at most 384 MiB of HBM per device.

```python
import jax
import jax.numpy as jnp
from jax import lax

C = 1920
HEIGHT = 32
WIDTH = 32
BATCH = 4
K = 17280
M = 4096


def draw_covariance(key, part):
    first = jax.random.fold_in(key, 11)
    second = jax.random.fold_in(key, 23)
    noise = jax.random.truncated_normal(first, -4.0, 4.0, (K, K), jnp.float32) * 0.01
    diagonal = jax.random.uniform(second, (K,), jnp.float32, 0.5, 1.5)
    symmetric = (noise + noise.T) * 0.7071
    positions = jnp.arange(K)
    on_diagonal = positions[:, None] == positions[None, :]
    return jnp.where(on_diagonal, diagonal[:, None], symmetric).astype(jnp.float32)


def block_scale(own_key, shape, shards, smallest, largest):
    def one(axis_at, blocks):
        draws = jax.random.uniform(jax.random.fold_in(jax.random.fold_in(own_key, 6), axis_at), (blocks,), jnp.float32, smallest / len(shards), largest / len(shards))
        return jnp.repeat(jnp.exp(draws), shape[axis_at] // blocks).reshape((-1,) + (1,) * (len(shape) - axis_at - 1))

    loudness = one(*shards[0])
    for cut in shards[1:]:
        loudness = loudness * one(*cut)
    return loudness


def gaussian(stream_key, dims, scale, reach, cuts=(), kind=jnp.bfloat16):
    values = scale * jax.random.normal(stream_key, dims, jnp.float32)
    if cuts:
        values = values * block_scale(stream_key, dims, cuts, -0.22, 0.18)
    return jnp.clip(values, -reach, reach).astype(kind)


def setup_inputs(seed: int = 0) -> dict:
    key_of = jax.random.split(jax.random.key(seed), 3)
    return {
        "activations": gaussian(key_of[0], (BATCH, HEIGHT, WIDTH, C), 1.0, 6.0, ((1, 4), (3, 8))),
        "covariance": draw_covariance(jax.random.fold_in(key_of[2], 71), 0),
    }


decay_rate = 0.9


def extract(padded, rows_out, cols_out):
    tap_views = []
    for row_tap in range(3):
        for col_tap in range(3):
            tap_views.append(padded[:, row_tap:row_tap + rows_out, col_tap:col_tap + cols_out, :])
    stacked = jnp.stack(tap_views, axis=-1)
    shape = stacked.shape
    return stacked.reshape(shape[0] * shape[1] * shape[2], shape[3] * shape[4])


def reference(activations, covariance):
    padded = jnp.pad(activations, ((0, 0), (1, 1), (1, 1), (0, 0)))
    patches = extract(padded, HEIGHT, WIDTH)
    gram = lax.dot_general(patches, patches, (((0,), (0,)), ((), ())), preferred_element_type=jnp.float32)
    return decay_rate * covariance + ((1.0 - decay_rate) / M) * gram
```

```python
import functools

import jax
import jax.numpy as jnp
from jax import lax
from jax.experimental import pallas as pl
from jax.experimental.pallas import tpu as pltpu
from jax.sharding import PartitionSpec as P

decay_rate = 0.9


def expand_kernel(width, height, image_ref, out_ref, spread):
    group, positions = image_ref.shape
    image = image_ref[...].astype(jnp.float32)
    place = lax.broadcasted_iota(jnp.int32, (8, positions), 1)
    column = place % width
    row = (place // width) % height
    row_ok = [row >= 1, None, row < height - 1]
    column_ok = [column >= 1, None, column < width - 1]
    for a in range(3):
        for b in range(3):
            offset = (a - 1) * width + (b - 1)
            moved = pltpu.roll(image, (-offset) % positions, 1) if offset else image
            keep = row_ok[a]
            if column_ok[b] is not None:
                keep = column_ok[b] if keep is None else keep & column_ok[b]
            for half in range(group // 8):
                part = moved[half * 8 : half * 8 + 8]
                if keep is not None:
                    part = jnp.where(keep, part, 0.0)
                for tile in range(positions // 128):
                    spread[tile, pl.ds(half * 72 + 3 * a + b, 8, stride=9), :] = part[
                        :, tile * 128 : tile * 128 + 128
                    ]
    for tile in range(positions // 128):
        out_ref[:, tile * 128 : tile * 128 + 128] = spread[tile].astype(jnp.bfloat16)


def expand(image, width, height):
    channels, positions = image.shape
    group = 16 if channels % 16 == 0 else 8
    return pl.pallas_call(
        functools.partial(expand_kernel, width, height),
        grid=(channels // group,),
        out_shape=jax.ShapeDtypeStruct((channels * 9, positions), jnp.bfloat16),
        in_specs=[pl.BlockSpec((group, positions), lambda i: (i, 0))],
        out_specs=pl.BlockSpec((group * 9, positions), lambda i: (i, 0)),
        scratch_shapes=[pltpu.VMEM((positions // 128, group * 9, 128), jnp.float32)],
        cost_estimate=pl.CostEstimate(
            flops=channels * 9 * positions * 20,
            bytes_accessed=channels * positions * 20,
            transcendentals=0,
        ),
    )(image)


def update_kernel(width, height, new_share, image_ref, edge_ref, patches_ref, low_ref, side_ref, covariance_ref, *rest):
    out_ref, corners, gram, spread = rest[-4:]
    group, positions = image_ref.shape
    columns = covariance_ref.shape[1]
    tiles = -(-columns // 128)
    image = image_ref[...].astype(jnp.float32)
    place = lax.broadcasted_iota(jnp.int32, (1, positions), 1)
    column = place % width
    row = (place // width) % height
    row_ok = [row >= 1, None, row < height - 1]
    column_ok = [column >= 1, None, column < width - 1]
    planes = []
    for a, b in ((0, 0), (0, 2), (2, 0), (2, 2)):
        offset = (a - 1) * width + (b - 1)
        moved = pltpu.roll(image, (-offset) % positions, 1)
        planes.append(jnp.where(row_ok[a] & column_ok[b], moved, 0.0))
    corners[...] = jnp.concatenate(planes, axis=0).astype(jnp.bfloat16)
    contract = (((1,), (1,)), ((), ()))
    gram[0 : 4 * group, 128 : 128 + columns] = lax.dot_general(
        corners[...], patches_ref[...], contract, preferred_element_type=jnp.float32
    )
    size = low_ref.shape[1]
    edge = edge_ref[...].astype(jnp.float32)
    edge = [edge[:, k * size : k * size + size] for k in (0, 2, 3, 4, 5)]
    low = lax.dot_general(
        jnp.concatenate(edge[:2], axis=0).astype(jnp.bfloat16), low_ref[...], contract, preferred_element_type=jnp.float32
    )
    gram[4 * group : 6 * group, 128 : 128 + columns] = low
    side = lax.dot_general(
        jnp.concatenate(edge[2:], axis=0).astype(jnp.bfloat16), side_ref[...], contract, preferred_element_type=jnp.float32
    )
    gram[6 * group : 9 * group, 128 : 128 + columns] = side

    def shifted(plane, tile, by):
        near = gram[plane * group : plane * group + group, tile * 128 : tile * 128 + 384]
        return pltpu.roll(near, by % 384, 1)[:, 128:256]

    for tile in range(tiles):
        tap = (lax.broadcasted_iota(jnp.int32, (1, 128), 1) + tile * 128) % 9
        here = slice(128 + tile * 128, 256 + tile * 128)
        for b in range(2):
            mine = slice((4 + b) * group, (5 + b) * group)
            gram[mine, here] = gram[mine, here] + jnp.where(
                tap < 3, shifted(2 + b, tile, -3), shifted(b, tile, 3)
            )
    first = (0, 4, 2)
    for tile in range(tiles):
        lane = lax.broadcasted_iota(jnp.int32, (1, 128), 1) + tile * 128
        here = slice(128 + tile * 128, 256 + tile * 128)
        for a in range(3):
            left = first[a]
            middle = gram[(6 + a) * group : (7 + a) * group, here] + jnp.where(
                lane % 3 == 0, shifted(left + 1, tile, -1), shifted(left, tile, 1)
            )
            taps = (
                gram[left * group : (left + 1) * group, here],
                middle,
                gram[(left + 1) * group : (left + 2) * group, here],
            )
            for b in range(3):
                spread[tile, pl.ds(3 * a + b, group, stride=9), :] = taps[b]
        end = min(columns, tile * 128 + 128)
        cut = slice(tile * 128, end)
        out_ref[:, cut] = (
            decay_rate * covariance_ref[:, cut] + new_share * spread[tile][:, : end - tile * 128]
        )


def update(image, edges, patches, low, side, covariance, group, first, steps, slabs, so_far, width, height):
    channels, positions = image.shape
    columns = covariance.shape[1]
    each = covariance.shape[0] // (9 * group * slabs)
    padded = -(-columns // 128) * 128 + 256
    whole = lambda i: (0, 0)
    once = pl.Buffered(1)
    tile = pl.BlockSpec(
        (group * 9, columns), lambda i: ((i // steps) * each + first + i % steps, 0)
    )
    operands = [image, edges, patches, low, side, covariance]
    specs = [
        pl.BlockSpec((group, positions), lambda i: (i, 0)),
        pl.BlockSpec((group, edges.shape[1]), lambda i: (i, 0)),
        pl.BlockSpec(patches.shape, whole, pipeline_mode=once),
        pl.BlockSpec(low.shape, whole, pipeline_mode=once),
        pl.BlockSpec(side.shape, whole, pipeline_mode=once),
        tile,
    ]
    aliases = {}
    if so_far is not None:
        operands.append(so_far)
        specs.append(pl.BlockSpec(memory_space=pl.ANY))
        aliases = {6: 0}
    return pl.pallas_call(
        functools.partial(update_kernel, width, height, (1.0 - decay_rate) / positions),
        grid=(slabs * steps,),
        out_shape=jax.ShapeDtypeStruct(covariance.shape, jnp.float32),
        in_specs=specs,
        out_specs=tile,
        scratch_shapes=[
            pltpu.VMEM((4 * group, positions), jnp.bfloat16),
            pltpu.VMEM((9 * group, padded), jnp.float32),
            pltpu.VMEM((-(-columns // 128), group * 9, 128), jnp.float32),
        ],
        input_output_aliases=aliases,
        cost_estimate=pl.CostEstimate(
            flops=2 * 4 * channels * positions * columns,
            bytes_accessed=channels * 9 * columns * 8 + patches.size * 2,
            transcendentals=0,
        ),
        compiler_params=pltpu.CompilerParams(vmem_limit_bytes=62 * 1024 * 1024),
    )(*operands)


def edge_selector(batch, height, width):
    place = lax.broadcasted_iota(jnp.int32, (batch * height * width, 1), 0)
    parts = []
    for size, last, stride in ((width, (height - 1) * width, 1), (height, width - 1, width)):
        line = lax.broadcasted_iota(jnp.int32, (1, batch * size), 1)
        for k in (-1, 0, 1):
            at = line % size + k
            wanted = (line // size) * height * width + last + at * stride
            parts.append((place == wanted) & (at >= 0) & (at < size))
    return jnp.concatenate(parts, axis=1).astype(jnp.bfloat16)


def edge_values(image, selector):
    return lax.dot_general(
        image, selector, (((1,), (0,)), ((), ())), preferred_element_type=jnp.float32
    ).astype(jnp.bfloat16)


def interleave(planes):
    empty = jnp.zeros_like(next(iter(planes.values())))
    stacked = jnp.stack([planes.get(t, empty) for t in range(9)], axis=1)
    return stacked.reshape(-1, stacked.shape[2])


def shards(activations, covariance):
    wide_count = lax.axis_size("wide")
    narrow_count = lax.axis_size("narrow")
    repeats = narrow_count // wide_count
    batch, rows, width, channels = activations.shape
    height = rows * wide_count
    strip = jnp.transpose(activations.reshape(batch * rows * width, channels)).reshape(
        channels, batch, rows * width
    )
    moves = []
    for r in range(wide_count):
        for s in range(narrow_count):
            target = (s // repeats) * narrow_count + r + (s % repeats) * wide_count
            moves.append((r * narrow_count + s, target))
    row_strip = lax.ppermute(strip, ("wide", "narrow"), moves)
    group = max(g for g in range(8, 49, 8) if channels % g == 0)
    steps = channels // group
    cuts = [0, (steps * 2) // 5, steps] if steps > 3 else [0, steps]
    positions = batch * height * width
    column_strips = lax.all_gather(strip, "wide")
    row_parts = []
    for low_cut, high_cut in zip(cuts[:-1], cuts[1:]):
        piece = row_strip[low_cut * group : high_cut * group]
        if row_parts:
            piece, row_parts[-1] = lax.optimization_barrier((piece, row_parts[-1]))
        row_parts.append(lax.all_gather(piece, "narrow"))
    selector = edge_selector(batch, height, width)
    column_image = jnp.transpose(column_strips, (1, 2, 0, 3)).reshape(channels, positions)
    patches = expand(column_image, width, height)
    edges = edge_values(column_image, selector)
    size = edges.shape[1] // 6
    edge = [edges[:, k * size : k * size + size] for k in range(6)]
    low = interleave({3 + b: edge[b] for b in range(3)})
    side = interleave({3 * a + 1: edge[3 + a] for a in range(3)})
    updated = None
    for part, first in enumerate(cuts[:-1]):
        count = cuts[part + 1] - first
        own = count * group
        image = jnp.transpose(
            row_parts[part].reshape(repeats, wide_count, own, batch, rows * width), (0, 2, 3, 1, 4)
        ).reshape(repeats * own, positions)
        edges = edge_values(image, selector)
        updated = update(
            image, edges, patches, low, side, covariance, group, first, count, repeats, updated, width, height
        )
    return updated


def solution(mesh):
    return jax.shard_map(
        shards,
        mesh=mesh,
        in_specs=(P(None, "wide", None, "narrow"), P("wide", "narrow")),
        out_specs=P("wide", "narrow"),
        check_vma=False,
    )
```
